32 devices in a mesh: depth: 8 (over z, y), lat: 4 (over x, core).
Axes of the slice: x: 2, y: 2, z: 4, core: 2. Of those that a mesh axis runs over, the one named last changes fastest.
Arguments:
- right_sides: bfloat16 [16, 2, 64, 3072], P('depth', None, None, 'lat'), may hold values from -6 to 6
- sources: int32 [64], replicated, may hold values from 0 to 3071
- coupling: float32 [16, 3072], P('depth', 'lat'), may hold values from 0.76 to 0.86
- block_cols: int32 [16, 24, 4], P('depth', 'lat'), may hold values from 0 to 23, as said below
- factors: bfloat16 [16, 24, 4, 2, 128, 128], P('depth', 'lat'), may hold values from -0.2 to 1.2
Outputs:
- solution: bfloat16 [16, 2, 64, 3072], P('depth', None, None, 'lat')
The draws below stay inside these ranges and needn't reach their ends.
Inputs may be any that keep to these rules, and one draw needn't show every extreme that they name: block_cols[k, r, 0] is r; the entries of a row are distinct and within 3 of r.
All inputs are finite; a program needn't handle non-finite values.
Results may differ from the reference program's by a relative error of at most 0.03.
Values may be sent and summed in bfloat16 or wider, within the bound.
A program may use at most 64 MiB of HBM per device.

```python
import math
import jax
import jax.numpy as jnp
from jax import lax

BLOCK = 128
NNZ = 4
REACH = 3
SHOTS = 64
NBLK = 24
PLANE = 3072
LAYERS = 16


def draw_coupling(key, part):
    shape = (LAYERS, PLANE)
    unit = jax.random.uniform(key, shape, jnp.float32, 0.0, 1.0)
    values = 0.76 + 0.1 * unit
    return jnp.clip(values, 0.76, 0.86).astype(jnp.float32)


def draw_block_cols(key, part):
    width = 2 * REACH + 1
    offsets = jnp.arange(width, dtype=jnp.int32) - REACH
    row_ids = jnp.arange(NBLK, dtype=jnp.int32)
    candidate = jnp.broadcast_to(row_ids[None, :, None] + offsets[None, None, :], (LAYERS, NBLK, width))
    noise = jax.random.randint(key, (LAYERS, NBLK, width), 0, 1000)
    score = noise * width + jnp.arange(width, dtype=jnp.int32)[None, None, :]
    inside = (candidate >= 0) & (candidate < NBLK)
    score = jnp.where(offsets[None, None, :] == 0, 10000000, jnp.where(inside, score, -1))
    _, chosen = lax.top_k(score, NNZ)
    return jnp.take_along_axis(candidate, chosen, axis=-1).astype(jnp.int32)


def draw_factors(key, part):
    shape = (LAYERS, NBLK, NNZ, 2, BLOCK, BLOCK)
    sigma = 0.5 / math.sqrt(2.0 * NNZ * BLOCK)
    noise = jax.random.normal(key, shape, jnp.float32) * sigma
    noise = jnp.clip(noise, -6.0 * sigma, 6.0 * sigma)
    identity = jnp.eye(BLOCK, dtype=jnp.float32)
    leading = ((jnp.arange(NNZ) == 0)[:, None] & (jnp.arange(2) == 0)[None, :]).astype(jnp.float32)
    return (noise + leading[None, None, :, :, None, None] * identity).astype(jnp.bfloat16)


def plant(entries, key, low, largest):
    longest = entries.shape.index(max(entries.shape))
    spots = []
    for shift in (0, 1):
        where = [jax.random.randint(jax.random.fold_in(key, axis), (), 0, length) for axis, length in enumerate(entries.shape)]
        where[longest] = (where[longest] + shift) % entries.shape[longest]
        spots.append(tuple(where))
    return entries.at[spots[0]].set(low).at[spots[1]].set(largest)


def block_scale(key, dims, cuts, low, largest):
    def one(position, shards_of):
        steps = jax.random.uniform(jax.random.fold_in(jax.random.fold_in(key, 6), position), (shards_of,), jnp.float32, low / len(cuts), largest / len(cuts))
        return jnp.repeat(jnp.exp(steps), dims[position] // shards_of).reshape((-1,) + (1,) * (len(dims) - position - 1))

    loudness = one(*cuts[0])
    for cut in cuts[1:]:
        loudness = loudness * one(*cut)
    return loudness


def gaussian(rng, shape, scale, reach, cuts=(), held_as=jnp.bfloat16):
    factor_of = block_scale(rng, shape, cuts, -0.22, 0.18) if cuts else 1.0
    values = jax.random.normal(rng, shape, jnp.float32) * scale * factor_of
    return jnp.minimum(jnp.maximum(values, -reach), reach).astype(held_as)


def setup_inputs(seed: int = 0) -> dict:
    arg_keys = jax.random.split(jax.random.key(seed), 6)
    return {
        "right_sides": gaussian(arg_keys[0], (LAYERS, 2, SHOTS, PLANE), 1.0, 6.0, ((0, 8), (3, 4))),
        "sources": plant(jax.random.randint(arg_keys[1], (SHOTS,), 0, PLANE), jax.random.fold_in(arg_keys[1], 1), 0, PLANE - 1).astype(jnp.int32),
        "coupling": draw_coupling(jax.random.fold_in(arg_keys[5], 71), 0),
        "block_cols": draw_block_cols(jax.random.fold_in(arg_keys[5], 71), 0),
        "factors": draw_factors(jax.random.fold_in(arg_keys[5], 71), 0),
    }


source_gain = 8.0


def apply_whole(vector, columns, factor_set):
    shot_count = vector.shape[1]
    padding = REACH * BLOCK
    extended = jnp.pad(vector.astype(jnp.float32), ((0, 0), (0, 0), (padding, padding)))
    pieces = extended.reshape(2, shot_count, -1, BLOCK)
    index = (columns + REACH).reshape(-1).astype(jnp.int32)
    picked = jnp.take(pieces, index, axis=2).reshape(2, shot_count, NBLK, NNZ, BLOCK)
    product = jnp.einsum("psrnj,rnqji->pqsri", picked, factor_set.astype(jnp.float32), precision=lax.Precision.HIGHEST)
    real_part = product[0, 0] - product[1, 1]
    imag_part = product[0, 1] + product[1, 0]
    return jnp.stack([real_part, imag_part]).reshape(2, shot_count, PLANE)


def reference(right_sides, sources, coupling, block_cols, factors):
    spike = jnp.zeros((SHOTS, PLANE), jnp.float32).at[jnp.arange(SHOTS), sources].set(source_gain)

    def down_step(previous, items):
        layer_rhs, couple_row, columns, factor_set = items
        source_load = layer_rhs.astype(jnp.float32)
        source_load = source_load.at[0].add(spike)
        mixed_in = (source_load - couple_row[None, None, :] * previous.astype(jnp.float32)).astype(jnp.bfloat16)
        result = apply_whole(mixed_in, columns, factor_set).astype(jnp.bfloat16)
        return result, result

    start = jnp.zeros((2, SHOTS, PLANE), jnp.bfloat16)
    _, stored = lax.scan(down_step, start, (right_sides, coupling, block_cols, factors))

    def up_step(carried, items):
        down_field, couple_row, columns, factor_set = items
        updated = (down_field.astype(jnp.float32) - apply_whole(carried, columns, factor_set)).astype(jnp.bfloat16)
        handed = (couple_row[None, None, :] * updated.astype(jnp.float32)).astype(jnp.bfloat16)
        return handed, updated

    _, solution = lax.scan(up_step, start, (stored, coupling, block_cols, factors), reverse=True)
    return solution
```

```python
import functools

import jax
import jax.numpy as jnp
from jax import lax
from jax.experimental import pallas as pl
from jax.experimental.pallas import tpu as pltpu
from jax.sharding import PartitionSpec as P

REACH = 3
FRONTS = 4

source_gain = 8.0

MESH = pl.DeviceIdType.MESH


def sweep_kernel(
    depth_count, lat_count, fronts,
    cols_ref, srcs_ref, rhs_ref, coup_ref, fac_ref, out_ref,
    ext, din, uin, dmid, umid, wa, wb, mixed, handed, hout, rhalo, chalo,
    d_send, d_recv, u_send, u_recv, dm_send, dm_recv, um_send, um_recv, p_send, p_recv,
):
    d = lax.axis_index("depth")
    l = lax.axis_index("lat")
    rows, stored, _, blk, _ = fac_ref.shape[1:]
    shots = rhs_ref.shape[2] // fronts
    ext_rows = rows + 2 * REACH
    halo = REACH * blk

    def valid(dd, dl):
        ok = jnp.bool_(True)
        if dd < 0:
            ok = d > 0
        if dd > 0:
            ok = d < depth_count - 1
        if dl < 0:
            ok = ok & (l > 0)
        if dl > 0:
            ok = ok & (l < lat_count - 1)
        return ok

    around = [(dd, dl) for dd in (-1, 0, 1) for dl in (-1, 0, 1) if (dd, dl) != (0, 0)]
    barrier = pltpu.get_barrier_semaphore()
    total = jnp.int32(0)
    for dd, dl in around:
        ok = valid(dd, dl)

        @pl.when(ok)
        def _():
            pl.semaphore_signal(barrier, inc=1, device_id=(d + dd, l + dl), device_id_type=MESH)

        total = total + ok.astype(jnp.int32)
    pl.semaphore_wait(barrier, total)

    def remote(src, dst, ssem, rsem, dd, dl):
        return pltpu.make_async_remote_copy(
            src_ref=src, dst_ref=dst, send_sem=ssem, recv_sem=rsem,
            device_id=(d + dd, l + dl), device_id_type=MESH,
        )

    def pre_copy(side, which):
        dl = 1 if side == 0 else -1
        lanes = pl.ds(rows * blk - halo, halo) if side == 0 else pl.ds(0, halo)
        if which == 0:
            src, dst = rhs_ref.at[0, :, :, lanes], rhalo.at[side]
        else:
            src, dst = coup_ref.at[:, lanes], chalo.at[side]
        i = 2 * side + which
        return remote(src, dst, p_send.at[i], p_recv.at[i], 0, dl)

    def mid_copy(f, side, src, dst, ssem, rsem):
        dl = 1 if side == 0 else -1
        first = rows - REACH if side == 0 else 0
        return remote(
            src.at[f, pl.ds(first, REACH)], dst.at[f, side], ssem.at[f, side], rsem.at[f, side], 0, dl
        )

    def depth_copy(f, slot, src, dst, ssem, rsem, dd):
        dl = 1 - slot
        if slot == 0:
            a, b, n = rows - REACH, 0, REACH
        elif slot == 1:
            a, b, n = 0, REACH, rows
        else:
            a, b, n = 0, REACH + rows, REACH
        return remote(
            src.at[f, pl.ds(a, n)], dst.at[f, pl.ds(b, n)], ssem.at[f, slot], rsem.at[f, slot], dd, dl
        )

    def to_dl(side):
        return 1 if side == 0 else -1

    for side in (0, 1):
        @pl.when(valid(0, to_dl(side)))
        def _():
            for which in (0, 1):
                pre_copy(side, which).start()

    lane = lax.broadcasted_iota(jnp.int32, (shots, blk), 1)
    first_cell = (l * rows - REACH) * blk

    def load_of(front, rhs, e):
        srcs = srcs_ref[front, :]
        spike = jnp.where(srcs == first_cell + e * blk + lane, source_gain, 0.0).astype(jnp.float32)
        value = rhs.astype(jnp.float32)
        return jnp.concatenate([value[0] + spike, value[1]], axis=0)

    def apply_row(layer, r):
        picks = [cols_ref[layer, r * stored + n] - l * rows + REACH for n in range(stored)]
        xs = [ext[jnp.clip(pick, 0, ext_rows - 1)] for pick in picks]
        x = jnp.concatenate(xs, axis=1)
        w = jnp.concatenate(
            [jnp.concatenate([fac_ref[layer, r, n, 0], fac_ref[layer, r, n, 1]], axis=1) for n in range(stored)],
            axis=0,
        )
        p = jnp.dot(x, w, preferred_element_type=jnp.float32)
        real = p[:shots, :blk] - p[shots:, blk:]
        imag = p[:shots, blk:] + p[shots:, :blk]
        return jnp.concatenate([real, imag], axis=0)

    def coup_of(layer, r):
        return coup_ref[pl.ds(layer, 1), pl.ds(r * blk, blk)]

    def depth_wait(f, dst, src, ssem, rsem, dd):
        for slot in (1, 0, 2):
            @pl.when(valid(dd, slot - 1))
            def _():
                depth_copy(f, slot, src, dst, ssem, rsem, -dd).wait_recv()

    def depth_start(f, dst, src, ssem, rsem, dd):
        for slot in (0, 2, 1):
            @pl.when(valid(dd, 1 - slot))
            def _():
                depth_copy(f, slot, src, dst, ssem, rsem, dd).start()

    def mid_start(f, src, dst, ssem, rsem):
        for side in (0, 1):
            @pl.when(valid(0, to_dl(side)))
            def _():
                mid_copy(f, side, src, dst, ssem, rsem).start()

    def mid_finish(f, src, dst, ssem, rsem):
        for r in range(rows):
            ext[REACH + r] = src[f, r]
        for side in (0, 1):
            @pl.when(valid(0, -to_dl(side)))
            def _():
                mid_copy(f, side, src, dst, ssem, rsem).wait_recv()
                for i in range(REACH):
                    e = i if side == 0 else REACH + rows + i
                    ext[e] = dst[f, side, i]

    def front_of(f):
        return pl.ds(pl.multiple_of(f * shots, shots), shots)

    def down_first(f):
        front = front_of(f)
        depth_wait(f, din, wb, d_send, d_recv, -1)

        def put(e, rhs, coup):
            previous = jnp.where(d > 0, din[f, e].astype(jnp.float32), 0.0)
            ext[e] = (load_of(front, rhs, e) - coup * previous).astype(jnp.bfloat16)

        for r in range(rows):
            put(REACH + r, rhs_ref[0, :, front, pl.ds(r * blk, blk)], coup_of(0, r))
        for side in (0, 1):
            @pl.when(valid(0, -to_dl(side)))
            def _():
                for i in range(REACH):
                    cells = pl.ds(i * blk, blk)
                    e = i if side == 0 else REACH + rows + i
                    put(e, rhalo[side, :, front, cells], chalo[side, pl.ds(0, 1), cells])
        for r in range(rows):
            w = apply_row(0, r).astype(jnp.bfloat16)
            wa[f, r] = w
            load = load_of(front, rhs_ref[1, :, front, pl.ds(r * blk, blk)], REACH + r)
            mixed[f, r] = (load - coup_of(1, r) * w.astype(jnp.float32)).astype(jnp.bfloat16)
        mid_start(f, mixed, dmid, dm_send, dm_recv)

    def down_second(f):
        mid_finish(f, mixed, dmid, dm_send, dm_recv)
        for r in range(rows):
            wb[f, r] = apply_row(1, r).astype(jnp.bfloat16)
        depth_start(f, din, wb, d_send, d_recv, 1)

    def emit(layer, f, r, value):
        s = value.astype(jnp.bfloat16)
        front = front_of(f)
        out_ref[layer, 0, front, pl.ds(r * blk, blk)] = s[:shots]
        out_ref[layer, 1, front, pl.ds(r * blk, blk)] = s[shots:]
        return (coup_of(layer, r) * s.astype(jnp.float32)).astype(jnp.bfloat16)

    def up_first(f):
        @pl.when(d < depth_count - 1)
        def _():
            depth_wait(f, uin, hout, u_send, u_recv, 1)
            for r in range(rows):
                ext[REACH + r] = uin[f, REACH + r]
            for side in (0, 1):
                @pl.when(valid(0, -to_dl(side)))
                def _():
                    for i in range(REACH):
                        e = i if side == 0 else REACH + rows + i
                        ext[e] = uin[f, e]
            for r in range(rows):
                handed[f, r] = emit(1, f, r, wb[f, r].astype(jnp.float32) - apply_row(1, r))

        @pl.when(d == depth_count - 1)
        def _():
            for r in range(rows):
                handed[f, r] = emit(1, f, r, wb[f, r].astype(jnp.float32))

        mid_start(f, handed, umid, um_send, um_recv)

    def up_second(f):
        mid_finish(f, handed, umid, um_send, um_recv)
        for r in range(rows):
            hout[f, r] = emit(0, f, r, wa[f, r].astype(jnp.float32) - apply_row(0, r))
        depth_start(f, uin, hout, u_send, u_recv, -1)

    for side in (0, 1):
        @pl.when(valid(0, -to_dl(side)))
        def _():
            for which in (0, 1):
                pre_copy(side, which).wait_recv()

    def pipeline(first, second):
        @pl.loop(0, fronts + 1)
        def _(t):
            @pl.when(t < fronts)
            def _():
                first(t)

            @pl.when(t > 0)
            def _():
                second(t - 1)

    pipeline(down_first, down_second)
    pipeline(up_first, up_second)

    for side in (0, 1):
        @pl.when(valid(0, to_dl(side)))
        def _():
            for which in (0, 1):
                pre_copy(side, which).wait_send()

    @pl.loop(0, fronts)
    def _(f):
        for side in (0, 1):
            @pl.when(valid(0, to_dl(side)))
            def _():
                mid_copy(f, side, mixed, dmid, dm_send, dm_recv).wait_send()
                mid_copy(f, side, handed, umid, um_send, um_recv).wait_send()
        for slot in (0, 1, 2):
            @pl.when(valid(1, 1 - slot))
            def _():
                depth_copy(f, slot, wb, din, d_send, d_recv, 1).wait_send()

            @pl.when(valid(-1, 1 - slot))
            def _():
                depth_copy(f, slot, hout, uin, u_send, u_recv, -1).wait_send()


def per_device(right_sides, sources, coupling, block_cols, factors):
    layers, parts, shot_count, cells = right_sides.shape
    rows, stored = block_cols.shape[1:]
    blk = factors.shape[-1]
    assert layers == 2 and rows >= REACH and parts == 2
    fronts = FRONTS
    pair = parts * (shot_count // fronts)
    ext_rows = rows + 2 * REACH
    bf16 = jnp.bfloat16
    spread = jnp.broadcast_to(sources[:, None], (shot_count, blk))
    vmem = pl.BlockSpec(memory_space=pltpu.VMEM)
    smem = pl.BlockSpec(memory_space=pltpu.SMEM)
    dma = pltpu.SemaphoreType.DMA
    return pl.pallas_call(
        functools.partial(sweep_kernel, lax.axis_size("depth"), lax.axis_size("lat"), fronts),
        out_shape=jax.ShapeDtypeStruct(right_sides.shape, bf16),
        in_specs=[smem, vmem, vmem, vmem, vmem],
        out_specs=vmem,
        scratch_shapes=[
            pltpu.VMEM((ext_rows, pair, blk), bf16),
            pltpu.VMEM((fronts, ext_rows, pair, blk), bf16),
            pltpu.VMEM((fronts, ext_rows, pair, blk), bf16),
            pltpu.VMEM((fronts, 2, REACH, pair, blk), bf16),
            pltpu.VMEM((fronts, 2, REACH, pair, blk), bf16),
            pltpu.VMEM((fronts, rows, pair, blk), bf16),
            pltpu.VMEM((fronts, rows, pair, blk), bf16),
            pltpu.VMEM((fronts, rows, pair, blk), bf16),
            pltpu.VMEM((fronts, rows, pair, blk), bf16),
            pltpu.VMEM((fronts, rows, pair, blk), bf16),
            pltpu.VMEM((2, parts, shot_count, REACH * blk), bf16),
            pltpu.VMEM((2, layers, REACH * blk), jnp.float32),
            dma((fronts, 3)), dma((fronts, 3)), dma((fronts, 3)), dma((fronts, 3)),
            dma((fronts, 2)), dma((fronts, 2)), dma((fronts, 2)), dma((fronts, 2)),
            dma((4,)), dma((4,)),
        ],
        compiler_params=pltpu.CompilerParams(collective_id=0, has_side_effects=True),
    )(block_cols.reshape(layers, rows * stored), spread, right_sides, coupling, factors)


def solution(mesh):
    in_specs = (
        P("depth", None, None, "lat"),
        P(),
        P("depth", "lat"),
        P("depth", "lat", None),
        P("depth", "lat", None, None, None, None),
    )
    out_specs = P("depth", None, None, "lat")
    return jax.shard_map(
        per_device, mesh=mesh, in_specs=in_specs, out_specs=out_specs, check_vma=False
    )
```
